512 devices in a mesh: rows: 64 (over z, y), cols: 8 (over x, core).
Axes of the slice: x: 4, y: 4, z: 16, core: 2. Of those that a mesh axis runs over, the one named last changes fastest.
Arguments:
- lower_pivot: bfloat16 [4, 2048, 4, 2048], P(None, 'rows', None, 'cols'), may hold values from -0.0625 to 0.0625
- lower_rest: bfloat16 [98304, 4, 2048], P('rows', None, 'cols'), may hold values from -0.0625 to 0.0625
- diag_inverse: bfloat16 [4, 2048, 2048], P(None, 'cols', 'rows'), may hold values from -0.125 to 0.125
- rhs_pivot: bfloat16 [4, 2048, 512], P(None, 'rows', 'cols'), may hold values from -6 to 6
- rhs_rest: bfloat16 [512, 98304], P('cols', 'rows'), may hold values from -6 to 6
Outputs:
- solution: bfloat16 [4, 2048, 512], P(None, 'cols')
- remainder: bfloat16 [512, 98304], P('cols', 'rows')
The draws below stay inside these ranges and needn't reach their ends.
All inputs are finite; a program needn't handle non-finite values.
Results may differ from the reference program's by a relative error of at most 0.017.
Values may be sent and summed in bfloat16 or wider, within the bound.
A program may use at most 64 MiB of HBM per device.

```python
import jax
import jax.numpy as jnp
from jax import lax

NB = 2048
NRHS = 512
NSTEP = 4
REST = 98304
N_COLS = 8


def levels(key, dims, shards, smallest, high):
    def one(axis_at, parts):
        draws = jax.random.uniform(jax.random.fold_in(jax.random.fold_in(key, 6), axis_at), (parts,), jnp.float32, smallest / len(shards), high / len(shards))
        return jnp.repeat(jnp.exp(draws), dims[axis_at] // parts).reshape((-1,) + (1,) * (len(dims) - axis_at - 1))

    factor_of = one(*shards[0])
    for cut in shards[1:]:
        factor_of = factor_of * one(*cut)
    return factor_of


def normal_values(rng, dims, spread, most, split=(), kind=jnp.bfloat16):
    drawn = spread * jax.random.normal(rng, dims, jnp.float32)
    if split:
        drawn = drawn * levels(rng, dims, split, -0.22, 0.18)
    return jnp.clip(drawn, -most, most).astype(kind)


def setup_inputs(seed: int = 0) -> dict:
    arg_keys = jax.random.split(jax.random.key(seed), 6)
    lower_pivot = normal_values(arg_keys[0], (NSTEP, NB, NSTEP, NB), (NSTEP * NB) ** -0.5, 0.0625, ((1, 64), (3, 8)))
    lower_rest = normal_values(arg_keys[1], (REST, NSTEP, NB), (NSTEP * NB) ** -0.5, 0.0625, ((0, 64), (2, 8)))
    diag_inverse = normal_values(arg_keys[2], (NSTEP, NB, NB), NB ** -0.5, 0.125, ((1, 8), (2, 64)))
    rhs_pivot = normal_values(arg_keys[3], (NSTEP, NB, NRHS), 1.0, 6.0, ((1, 64), (2, 8)))
    rhs_rest = normal_values(arg_keys[4], (NRHS, REST), 1.0, 6.0, ((0, 8), (1, 64)))
    return dict(lower_pivot=lower_pivot, lower_rest=lower_rest, diag_inverse=diag_inverse, rhs_pivot=rhs_pivot, rhs_rest=rhs_rest)


def reference(lower_pivot, lower_rest, diag_inverse, rhs_pivot, rhs_rest):
    solved = []
    for step_index in range(NSTEP):
        residual = rhs_pivot[step_index].astype(jnp.float32)
        if step_index > 0:
            factor_part = lower_pivot[step_index, :, :step_index, :].reshape(NB, step_index * NB)
            known_part = jnp.concatenate(solved, axis=0)
            residual = residual - jnp.dot(factor_part, known_part, preferred_element_type=jnp.float32)
        residual = residual.astype(jnp.bfloat16)
        solved.append(jnp.dot(diag_inverse[step_index], residual, preferred_element_type=jnp.float32).astype(jnp.bfloat16))
    solution = jnp.stack(solved)
    group_width = NB // N_COLS
    grouped_solution = solution.reshape(NSTEP, N_COLS, group_width, NRHS)
    grouped_lower = lower_rest.reshape(REST, NSTEP, N_COLS, group_width)
    total_sum = jnp.zeros((NRHS, REST), jnp.float32)
    for group_index in range(N_COLS):
        flat_solution = grouped_solution[:, group_index].reshape(NSTEP * group_width, NRHS)
        flat_lower = grouped_lower[:, :, group_index, :].reshape(REST, NSTEP * group_width)
        partial_sum = lax.dot_general(flat_solution, flat_lower, (((0,), (1,)), ((), ())), preferred_element_type=jnp.float32)
        rounded = lax.optimization_barrier(partial_sum.astype(jnp.bfloat16))
        total_sum = total_sum + rounded.astype(jnp.float32)
    remainder = (rhs_rest.astype(jnp.float32) - total_sum).astype(jnp.bfloat16)
    return solution, remainder
```

```python
import functools

import jax
import jax.numpy as jnp
from jax import lax
from jax.experimental import pallas as pl
from jax.experimental.pallas import tpu as pltpu
from jax.sharding import PartitionSpec as P

MESH = pl.DeviceIdType.MESH
BF = jnp.bfloat16
F32 = jnp.float32
NZ, NY, NX = 16, 4, 4
STARTS = (0, 2, 4, 7)
LENS = (2, 2, 3, 4)
BLOCKS = 11
CONTRACT_LAST = (((1,), (1,)), ((), ()))


def dot_t(a, b):
    return lax.dot_general(a, b, CONTRACT_LAST, preferred_element_type=F32)


def kernel(own, rr, lr_hbm, sol, rem, mats, xg, lr, csend, crecv, xbuf, ybuf, fsend, frecv, rsend, rbuf,
           lsem, msend, mrecv, gsend, grecv, csem, xsem, ysem, fsem, rsem):
    r = lax.axis_index("rows")
    c = lax.axis_index("cols")
    z, y = r // NY, lax.rem(r, NY)
    x, core = c // 2, lax.rem(c, 2)

    def dev(zz, yy, xx, cc):
        return (zz * NY + yy, xx * 2 + cc)

    def zmod(v):
        return lax.rem(v + 2 * NZ, NZ)

    zdev = (dev(zmod(z + 1), y, x, core), dev(zmod(z - 1), y, x, core))
    xdev = [dev(z, y, lax.rem(x + d, NX), core) for d in (1, 2, 3)]
    ydev = [dev(z, lax.rem(y + d, NY), x, core) for d in (1, 2, 3)]
    cdev = dev(z, y, x, 1 - core)

    barrier = pltpu.get_barrier_semaphore()
    peers = [zdev[0], zdev[1], cdev] + xdev + ydev
    for p in peers:
        pl.semaphore_signal(barrier, inc=1, device_id=p, device_id_type=MESH)
    load = pltpu.make_async_copy(lr_hbm, lr, lsem.at[0])
    load.start()
    pl.semaphore_wait(barrier, len(peers))

    pending = []

    def rows_of(zz):
        return pl.ds(pl.multiple_of(zz * 32, 32), 32)

    def mat_slice(s, zz):
        return mats.at[pl.ds(STARTS[s], LENS[s]), rows_of(zz), :]

    def send_mat(s, way, k):
        src_z = zmod(z - k) if way == 0 else zmod(z + k)
        src = own.at[pl.ds(STARTS[s], LENS[s])] if k == 0 else mat_slice(s, src_z)
        cp = pltpu.make_async_remote_copy(src, mat_slice(s, src_z), msend.at[s, way, k], mrecv.at[s, way, k],
                                          device_id=zdev[way], device_id_type=MESH)
        cp.start()
        pending.append(cp)

    def wait_mat(s, way, k):
        src_z = zmod(z - k - 1) if way == 0 else zmod(z + k + 1)
        sl = mat_slice(s, src_z)
        pltpu.make_async_remote_copy(sl, sl, msend.at[s, way, k], mrecv.at[s, way, k],
                                     device_id=zdev[way], device_id_type=MESH).wait_recv()

    def relay_mat(s, k):
        for way, last in ((0, 8), (1, 7)):
            if k <= last:
                wait_mat(s, way, k - 1)
                if k < last:
                    send_mat(s, way, k)

    for s in range(4):
        for way in range(2):
            send_mat(s, way, 0)
    keep = pltpu.make_async_copy(own, mats.at[:, rows_of(z), :], lsem.at[1])
    keep.start()
    keep.wait()

    for k in range(1, 9):
        for s in range(4):
            relay_mat(s, k)

    plane_col = z // 2
    base = lax.rem(z, 2) * 32
    lane = lax.broadcasted_iota(jnp.int32, (32, 256), 1)
    row = lax.broadcasted_iota(jnp.int32, (32, 256), 0)
    owner = plane_col == c

    def pick(s):
        hit = jnp.logical_and(lane == row + (s * 64 + base), jnp.broadcast_to(owner, lane.shape))
        return jnp.where(hit, 1.0, 0.0).astype(BF)

    for s in range(4):
        part = dot_t(pick(s), mats[0])
        for t in range(s):
            part = part - dot_t(xg[z, t], mats[STARTS[s] + 1 + t])
        csend[s] = part.astype(BF)
        ccp = pltpu.make_async_remote_copy(csend.at[s], crecv.at[s], csem.at[0, s], csem.at[1, s],
                                           device_id=cdev, device_id_type=MESH)
        ccp.start()
        pending.append(ccp)
        ccp.wait_recv()
        xbuf[s, x] = (csend[s].astype(F32) + crecv[s].astype(F32)).astype(BF)
        sent = []
        for d in (1, 2, 3):
            xcp = pltpu.make_async_remote_copy(xbuf.at[s, x], xbuf.at[s, x], xsem.at[0, s, d - 1], xsem.at[1, s, d - 1],
                                               device_id=xdev[d - 1], device_id_type=MESH)
            xcp.start()
            sent.append(xcp)
        for d in (1, 2, 3):
            sl = xbuf.at[s, lax.rem(x + NX - d, NX)]
            pltpu.make_async_remote_copy(sl, sl, xsem.at[0, s, d - 1], xsem.at[1, s, d - 1],
                                         device_id=xdev[d - 1], device_id_type=MESH).wait_recv()
        pending.extend(sent)
        total = xbuf[s, 0].astype(F32)
        for i in range(1, NX):
            total = total + xbuf[s, i].astype(F32)
        prod = jnp.dot(total.astype(BF), mats[STARTS[s] if s else 1], preferred_element_type=F32)
        ybuf[s, y] = prod.astype(BF)
        sent = []
        for d in (1, 2, 3):
            ycp = pltpu.make_async_remote_copy(ybuf.at[s, y], ybuf.at[s, y], ysem.at[0, s, d - 1], ysem.at[1, s, d - 1],
                                               device_id=ydev[d - 1], device_id_type=MESH)
            ycp.start()
            sent.append(ycp)
        for d in (1, 2, 3):
            sl = ybuf.at[s, lax.rem(y + NY - d, NY)]
            pltpu.make_async_remote_copy(sl, sl, ysem.at[0, s, d - 1], ysem.at[1, s, d - 1],
                                         device_id=ydev[d - 1], device_id_type=MESH).wait_recv()
        pending.extend(sent)
        solved = ybuf[s, 0].astype(F32)
        for i in range(1, NY):
            solved = solved + ybuf[s, i].astype(F32)
        xg[z, s] = solved.astype(BF)

    def send_x(way, k):
        src_z = zmod(z - k) if way == 0 else zmod(z + k)
        cp = pltpu.make_async_remote_copy(xg.at[src_z], xg.at[src_z], gsend.at[way, k], grecv.at[way, k],
                                          device_id=zdev[way], device_id_type=MESH)
        cp.start()
        pending.append(cp)

    def wait_x(way, k):
        src_z = zmod(z - k - 1) if way == 0 else zmod(z + k + 1)
        pltpu.make_async_remote_copy(xg.at[src_z], xg.at[src_z], gsend.at[way, k], grecv.at[way, k],
                                     device_id=zdev[way], device_id_type=MESH).wait_recv()

    send_x(0, 0)
    send_x(1, 0)
    for k in range(1, 9):
        for way, last in ((0, 8), (1, 7)):
            if k <= last:
                wait_x(way, k - 1)
                if k < last:
                    send_x(way, k)
    load.wait()

    mine = pl.ds(pl.multiple_of(core * 64, 64), 64)
    other = pl.ds(pl.multiple_of((1 - core) * 64, 64), 64)
    exchanged = []
    for i, e in enumerate((2, 1, 3, 0)):
        g = lax.rem(x + e, NX)
        acc = None
        for t in range(4):
            xs = xg[pl.ds(g * 4, 4), t].reshape(128, 256)
            term = dot_t(xs, lr[:, t * 256:(t + 1) * 256])
            acc = term if acc is None else acc + term
        fsend[i] = acc.astype(BF)
        cp = pltpu.make_async_remote_copy(fsend.at[i, other], frecv.at[i], fsem.at[0, i], fsem.at[1, i],
                                          device_id=cdev, device_id_type=MESH)
        cp.start()
        exchanged.append((i, e, cp))
    final = None
    for i, e, cp in exchanged:
        cp.wait_recv()
        pending.append(cp)
        chip = fsend[i, mine].astype(F32) + frecv[i].astype(F32)
        if e:
            rsend[i] = chip.astype(BF)
            rcp = pltpu.make_async_remote_copy(rsend.at[i], rbuf.at[e - 1], rsem.at[0, e - 1], rsem.at[1, e - 1],
                                               device_id=xdev[e - 1], device_id_type=MESH)
            rcp.start()
            pending.append(rcp)
        else:
            final = chip
    for g in range(4):
        for t in range(4):
            xs = xg[g * 4:g * 4 + 4, t].reshape(128, 256)
            sol[t, :, g * 128:(g + 1) * 128] = xs.T
    for e in (1, 3, 2):
        pltpu.make_async_remote_copy(rsend.at[0], rbuf.at[e - 1], rsem.at[0, e - 1], rsem.at[1, e - 1],
                                     device_id=xdev[e - 1], device_id_type=MESH).wait_recv()
        final = final + rbuf[e - 1].astype(F32)
    rem[...] = (rr[...].astype(F32) - final).astype(BF)
    for cp in pending:
        cp.wait_send()


def per_device(lower_pivot, lower_rest, diag_inverse, rhs_pivot, rhs_rest):
    dt = jnp.swapaxes(diag_inverse, 1, 2)
    blocks = [jnp.swapaxes(rhs_pivot, 0, 1).reshape(32, 256)]
    for s in range(4):
        blocks.append(dt[s])
        for t in range(s):
            blocks.append(lower_pivot[s, :, t, :])
    own = jnp.stack(blocks)
    lr = lower_rest.reshape(1536, 1024)
    vmem = pl.BlockSpec(memory_space=pltpu.VMEM)
    dma = pltpu.SemaphoreType.DMA
    sol, rem = pl.pallas_call(
        kernel,
        out_shape=(jax.ShapeDtypeStruct((4, 256, 512), BF), jax.ShapeDtypeStruct((64, 1536), BF)),
        in_specs=[vmem, vmem, pl.BlockSpec(memory_space=pl.ANY)],
        out_specs=(vmem, vmem),
        scratch_shapes=[
            pltpu.VMEM((BLOCKS, 512, 256), BF),
            pltpu.VMEM((NZ, 4, 32, 256), BF),
            pltpu.VMEM((1536, 1024), BF),
            pltpu.VMEM((4, 32, 512), BF),
            pltpu.VMEM((4, 32, 512), BF),
            pltpu.VMEM((4, 4, 32, 512), BF),
            pltpu.VMEM((4, 4, 32, 256), BF),
            pltpu.VMEM((4, 128, 1536), BF),
            pltpu.VMEM((4, 64, 1536), BF),
            pltpu.VMEM((4, 64, 1536), BF),
            pltpu.VMEM((3, 64, 1536), BF),
            dma((2,)),
            dma((4, 2, 8)),
            dma((4, 2, 8)),
            dma((2, 8)),
            dma((2, 8)),
            dma((2, 4)),
            dma((2, 4, 3)),
            dma((2, 4, 3)),
            dma((2, 4)),
            dma((2, 3)),
        ],
        compiler_params=pltpu.CompilerParams(
            collective_id=0, has_side_effects=True, vmem_limit_bytes=48 * 1024 * 1024
        ),
        name="substitution",
    )(own, rhs_rest, lr)
    return sol, rem


def solution(mesh):
    placed = (
        P(None, "rows", None, "cols"),
        P("rows", None, "cols"),
        P(None, "cols", "rows"),
        P(None, "rows", "cols"),
        P("cols", "rows"),
    )
    return jax.shard_map(
        per_device,
        mesh=mesh,
        in_specs=placed,
        out_specs=(P(None, "cols", None), P("cols", "rows")),
        check_vma=False,
    )
```

```python
import jax
import jax.numpy as jnp
from jax import lax
from jax.experimental import pallas as pl
from jax.experimental.pallas import tpu as pltpu
from jax.sharding import PartitionSpec as P

MESH = pl.DeviceIdType.MESH
BF = jnp.bfloat16
F32 = jnp.float32
NZ, NY, NX = 16, 4, 4
STARTS = (0, 1, 3, 6)
LENS = (1, 2, 3, 4)
BLOCKS = 10
OWN_HOPS = (5, -5, 2, -2, 1, -1)
CONTRACT_LAST = (((1,), (1,)), ((), ()))


def dot_t(a, b):
    return lax.dot_general(a, b, CONTRACT_LAST, preferred_element_type=F32)


def kernel(lp_hbm, dt_hbm, rp_hbm, rr_hbm, lr_hbm, sol, rem,
           lp, dt, rp, rr, lr_raw, lr, mats, bm, xg, xl, csend, crecv, xbuf, ybuf, acc, fsend, frecv, rsend, rbuf,
           lsem, msend, mrecv, wsend, wrecv, csem, xsem, ysem, qsem, fsem, rsem):
    r = lax.axis_index("rows")
    c = lax.axis_index("cols")
    z, y = r // NY, lax.rem(r, NY)
    x, core = c // 2, lax.rem(c, 2)

    def dev(zz, yy, xx, cc):
        return (zz * NY + yy, xx * 2 + cc)

    def zmod(v):
        return lax.rem(v + 2 * NZ, NZ)

    def zdev(o):
        return dev(zmod(z + o), y, x, core)

    xdev = [dev(z, y, lax.rem(x + d, NX), core) for d in (1, 2, 3)]
    ydev = [dev(z, lax.rem(y + d, NY), x, core) for d in (1, 2, 3)]
    cdev = dev(z, y, x, 1 - core)

    barrier = pltpu.get_barrier_semaphore()
    peers = [zdev(o) for o in (5, -5, 3, -3, 2, -2, 1, -1)] + xdev + ydev + [cdev]
    for p in peers:
        pl.semaphore_signal(barrier, inc=1, device_id=p, device_id_type=MESH)
    loads = [pltpu.make_async_copy(a, b, lsem.at[i]) for i, (a, b) in enumerate(
        ((rp_hbm, rp), (dt_hbm, dt), (lp_hbm, lp), (lr_hbm, lr_raw), (rr_hbm, rr)))]
    for ld in loads:
        ld.start()

    pending = []

    def rows_of(zz):
        return pl.ds(pl.multiple_of(zz * 32, 32), 32)

    def remote(src, dst, send, recv, to):
        cp = pltpu.make_async_remote_copy(src, dst, send, recv, device_id=to, device_id_type=MESH)
        cp.start()
        pending.append(cp)

    def arrive(dst, send, recv, to):
        pltpu.make_async_remote_copy(dst, dst, send, recv, device_id=to, device_id_type=MESH).wait_recv()

    def mat_slice(s, zz):
        return mats.at[pl.ds(STARTS[s], LENS[s]), rows_of(zz), :]

    def send_mat(s, way, k):
        sl = mat_slice(s, zmod(z - k) if way == 0 else zmod(z + k))
        remote(sl, sl, msend.at[s, way, k], mrecv.at[s, way, k], zdev(1 - 2 * way))

    def first(s):
        send_mat(s, 0, 0)
        send_mat(s, 1, 0)

    def relay(s, k):
        for way, last in ((0, 8), (1, 7)):
            if 1 <= k <= last:
                sl = mat_slice(s, zmod(z - k) if way == 0 else zmod(z + k))
                arrive(sl, msend.at[s, way, k - 1], mrecv.at[s, way, k - 1], zdev(1 - 2 * way))
                if k < last:
                    send_mat(s, way, k)

    quarter = pl.ds(pl.multiple_of(lax.rem(y, 2) * 16, 16), 16)

    def piece(w, zz):
        if w == 0:
            return xg.at[zz, y // 2, quarter, :]
        if w < 4:
            return xg.at[zz, w]
        return bm.at[w - 4, rows_of(zz), :] if w < 6 else mat_slice(w - 6, zz)

    def push(w, i, o, shard):
        sl = piece(w, zmod(z + shard))
        remote(sl, sl, wsend.at[w, i], wrecv.at[w, i], zdev(o))

    def got(w, i, o, shard):
        arrive(piece(w, zmod(z - o + shard)), wsend.at[w, i], wrecv.at[w, i], zdev(o))

    PASS = [(0, -5, (2, -2, 1, -1), 6), (1, 5, (-3, -2, 2, -1, 1), 10)]

    def wave_a(w):
        for i, o in enumerate(OWN_HOPS):
            push(w, i, o, 0)

    def wave_b(w):
        for i, shard, hops, base in PASS:
            got(w, i, OWN_HOPS[i], 0)
            for j, o in enumerate(hops):
                push(w, base + j, o, shard)

    def wave_c(w):
        for i in range(2, 6):
            got(w, i, OWN_HOPS[i], 0)
        for i, shard, hops, base in PASS:
            for j, o in enumerate(hops):
                got(w, base + j, o, shard)

    base_n = lax.rem(z, 2) * 32
    lane = lax.broadcasted_iota(jnp.int32, (32, 128), 1)
    row = lax.broadcasted_iota(jnp.int32, (32, 128), 0)
    owner = z // 2 == c

    def pick(s):
        hit = jnp.logical_and(lane == row + ((s % 2) * 64 + base_n), jnp.broadcast_to(owner, lane.shape))
        return jnp.where(hit, 1.0, 0.0).astype(BF)

    def step_p(s):
        part = dot_t(pick(s), bm[s // 2])
        for t in range(s):
            part = part - dot_t(xl[t], mats[STARTS[s] + 1 + t])
        csend[s] = part.astype(BF)
        remote(csend.at[s], crecv.at[s], csem.at[0, s], csem.at[1, s], cdev)

    def step_x(s):
        arrive(crecv.at[s], csem.at[0, s], csem.at[1, s], cdev)
        xbuf[s, x] = (csend[s].astype(F32) + crecv[s].astype(F32)).astype(BF)
        for d in (2, 1, 3):
            remote(xbuf.at[s, x], xbuf.at[s, x], xsem.at[0, s, d - 1], xsem.at[1, s, d - 1], xdev[d - 1])

    def step_y(s):
        for d in (1, 3, 2):
            arrive(xbuf.at[s, lax.rem(x + NX - d, NX)], xsem.at[0, s, d - 1], xsem.at[1, s, d - 1], xdev[d - 1])
        total = xbuf[s, 0].astype(F32)
        for i in range(1, NX):
            total = total + xbuf[s, i].astype(F32)
        prod = jnp.dot(total.astype(BF), mats[STARTS[s]], preferred_element_type=F32)
        ybuf[s, y] = prod.astype(BF)
        for d in (2, 1, 3):
            remote(ybuf.at[s, y], ybuf.at[s, y], ysem.at[0, s, d - 1], ysem.at[1, s, d - 1], ydev[d - 1])

    def step_z(s):
        for d in (1, 3, 2):
            arrive(ybuf.at[s, lax.rem(y + NY - d, NY)], ysem.at[0, s, d - 1], ysem.at[1, s, d - 1], ydev[d - 1])
        solved = ybuf[s, 0].astype(F32)
        for i in range(1, NY):
            solved = solved + ybuf[s, i].astype(F32)
        xl[s] = solved.astype(BF)
        if s == 1:
            xg[z, y // 2, quarter, :] = xl[y // 2, quarter, :]
            wave_a(0)
        elif s > 1:
            xg[z, s] = xl[s]
            wave_a(s)

    def share_slice(yy):
        return xg.at[:, yy // 2, pl.ds(pl.multiple_of(lax.rem(yy, 2) * 16, 16), 16), :]

    def share():
        for d in (2, 1, 3):
            remote(share_slice(y), share_slice(y), qsem.at[0, d - 1], qsem.at[1, d - 1], ydev[d - 1])

    def shared():
        for d in (1, 3, 2):
            arrive(share_slice(lax.rem(y + NY - d, NY)), qsem.at[0, d - 1], qsem.at[1, d - 1], ydev[d - 1])

    def tile(i):
        rows = pl.ds(i * 128, 128)
        for t in range(4):
            lr[rows, t * 256:(t + 1) * 256] = lr_raw[rows, t, :]

    loads[0].wait()
    for s in range(4):
        bm[s // 2, rows_of(z), (s % 2) * 64:(s % 2) * 64 + 64] = rp[s]
    loads[1].wait()
    loads[2].wait()
    for s in range(4):
        mats[STARTS[s], rows_of(z), :] = dt[s]
        for t in range(s):
            mats[STARTS[s] + 1 + t, rows_of(z), :] = lp[s, :, t, :]
    pl.semaphore_wait(barrier, len(peers))

    wave_a(4)
    wave_a(6)
    first(2)
    loads[3].wait()
    tile(0)
    tile(1)
    tile(2)
    tile(3)
    wave_b(4)
    wave_b(6)
    wave_a(7)
    relay(2, 1)
    first(3)
    tile(4)
    tile(5)
    tile(6)
    wave_c(4)
    step_p(0)
    relay(2, 2)
    step_x(0)
    wave_b(7)
    relay(3, 1)
    wave_c(6)
    step_y(0)
    wave_a(5)
    relay(2, 3)
    relay(3, 2)
    step_z(0)
    wave_c(7)
    step_p(1)
    relay(2, 4)
    step_x(1)
    wave_b(5)
    relay(3, 3)
    relay(2, 5)
    step_y(1)
    relay(3, 4)
    relay(2, 6)
    step_z(1)
    relay(2, 7)
    relay(3, 5)
    relay(2, 8)
    wave_c(5)
    step_p(2)
    relay(3, 6)
    step_x(2)
    wave_b(0)
    relay(3, 7)
    tile(7)
    tile(8)
    step_y(2)
    relay(3, 8)
    step_z(2)
    step_p(3)
    wave_c(0)
    share()
    tile(9)
    step_x(3)
    tile(10)
    tile(11)
    step_y(3)
    wave_b(2)
    step_z(3)
    shared()
    for i in range(4):
        rows = pl.ds(i * 128, 128)
        part = None
        for t in range(2):
            term = dot_t(xg[i * 4:i * 4 + 4, t].reshape(128, 256), lr[:, t * 256:(t + 1) * 256])
            part = term if part is None else part + term
        acc[rows, :] = part
    for g in range(4):
        for t in range(2):
            sol[t, :, g * 128:(g + 1) * 128] = xg[g * 4:g * 4 + 4, t].reshape(128, 256).T
    wave_b(3)
    wave_c(2)
    for i in range(4):
        rows = pl.ds(i * 128, 128)
        acc[rows, :] += dot_t(xg[i * 4:i * 4 + 4, 2].reshape(128, 256), lr[:, 512:768])
    for g in range(4):
        sol[2, :, g * 128:(g + 1) * 128] = xg[g * 4:g * 4 + 4, 2].reshape(128, 256).T
    wave_c(3)

    mine = pl.ds(pl.multiple_of(core * 64, 64), 64)
    other = pl.ds(pl.multiple_of((1 - core) * 64, 64), 64)
    order = (2, 1, 3, 0)
    for i, e in enumerate(order):
        g = lax.rem(x + e, NX)
        rows = pl.ds(pl.multiple_of(g * 128, 128), 128)
        part = acc[rows, :] + dot_t(xg[pl.ds(g * 4, 4), 3].reshape(128, 256), lr[:, 768:1024])
        fsend[i] = part.astype(BF)
        remote(fsend.at[i, other], frecv.at[i], fsem.at[0, i], fsem.at[1, i], cdev)
    final = None
    for i, e in enumerate(order):
        arrive(frecv.at[i], fsem.at[0, i], fsem.at[1, i], cdev)
        chip = fsend[i, mine].astype(F32) + frecv[i].astype(F32)
        if e:
            rsend[i] = chip.astype(BF)
            remote(rsend.at[i], rbuf.at[e - 1], rsem.at[0, e - 1], rsem.at[1, e - 1], xdev[e - 1])
        else:
            loads[4].wait()
            final = rr[...].astype(F32) - chip
    for g in range(4):
        sol[3, :, g * 128:(g + 1) * 128] = xg[g * 4:g * 4 + 4, 3].reshape(128, 256).T
    for e in (1, 3, 2):
        arrive(rbuf.at[e - 1], rsem.at[0, e - 1], rsem.at[1, e - 1], xdev[e - 1])
        final = final - rbuf[e - 1].astype(F32)
    rem[...] = final.astype(BF)
    for cp in pending:
        cp.wait_send()


def per_device(lower_pivot, lower_rest, diag_inverse, rhs_pivot, rhs_rest):
    vmem = pl.BlockSpec(memory_space=pltpu.VMEM)
    hbm = pl.BlockSpec(memory_space=pl.ANY)
    dma = pltpu.SemaphoreType.DMA
    return pl.pallas_call(
        kernel,
        out_shape=(jax.ShapeDtypeStruct((4, 256, 512), BF), jax.ShapeDtypeStruct((64, 1536), BF)),
        in_specs=[hbm] * 5,
        out_specs=(vmem, vmem),
        scratch_shapes=[
            pltpu.VMEM((4, 32, 4, 256), BF),
            pltpu.VMEM((4, 32, 256), BF),
            pltpu.VMEM((4, 32, 64), BF),
            pltpu.VMEM((64, 1536), BF),
            pltpu.VMEM((1536, 4, 256), BF),
            pltpu.VMEM((1536, 1024), BF),
            pltpu.VMEM((BLOCKS, 512, 256), BF),
            pltpu.VMEM((2, 512, 128), BF),
            pltpu.VMEM((NZ, 4, 32, 256), BF),
            pltpu.VMEM((4, 32, 256), BF),
            pltpu.VMEM((4, 32, 512), BF),
            pltpu.VMEM((4, 32, 512), BF),
            pltpu.VMEM((4, 4, 32, 512), BF),
            pltpu.VMEM((4, 4, 32, 256), BF),
            pltpu.VMEM((512, 1536), F32),
            pltpu.VMEM((4, 128, 1536), BF),
            pltpu.VMEM((4, 64, 1536), BF),
            pltpu.VMEM((3, 64, 1536), BF),
            pltpu.VMEM((3, 64, 1536), BF),
            dma((5,)),
            dma((4, 2, 8)),
            dma((4, 2, 8)),
            dma((8, 15)),
            dma((8, 15)),
            dma((2, 4)),
            dma((2, 4, 3)),
            dma((2, 4, 3)),
            dma((2, 3)),
            dma((2, 4)),
            dma((2, 3)),
        ],
        compiler_params=pltpu.CompilerParams(
            collective_id=0, has_side_effects=True, vmem_limit_bytes=63 * 1024 * 1024
        ),
        name="substitution",
    )(lower_pivot, jnp.swapaxes(diag_inverse, 1, 2), rhs_pivot, rhs_rest, lower_rest)


def solution(mesh):
    placed = (
        P(None, "rows", None, "cols"),
        P("rows", None, "cols"),
        P(None, "cols", "rows"),
        P(None, "rows", "cols"),
        P("cols", "rows"),
    )
    return jax.shard_map(
        per_device,
        mesh=mesh,
        in_specs=placed,
        out_specs=(P(None, "cols", None), P("cols", "rows")),
        check_vma=False,
    )
```

```python
import jax
import jax.numpy as jnp
from jax import lax
from jax.experimental import pallas as pl
from jax.experimental.pallas import tpu as pltpu
from jax.sharding import PartitionSpec as P

MESH = pl.DeviceIdType.MESH
BF = jnp.bfloat16
F32 = jnp.float32
NZ, NY, NX = 16, 4, 4
STARTS = (0, 1, 3, 6)
LENS = (1, 2, 3, 4)
BLOCKS = 10
OWN_HOPS = (5, -5, 2, -2, 1, -1)
CONTRACT_LAST = (((1,), (1,)), ((), ()))


def dot_t(a, b):
    return lax.dot_general(a, b, CONTRACT_LAST, preferred_element_type=F32)


def kernel(lp_hbm, dt_hbm, rp_hbm, rr_hbm, lr_hbm, sol, rem,
           lp, dt, rp, rr, lr_raw, lr, mats, bm, xg, xl, csend, crecv, xbuf, ybuf, acc, fsend, frecv, rsend, rbuf,
           lsem, msend, mrecv, wsend, wrecv, csem, xsem, ysem, qsem, fsem, rsem):
    r = lax.axis_index("rows")
    c = lax.axis_index("cols")
    z, y = r // NY, lax.rem(r, NY)
    x, core = c // 2, lax.rem(c, 2)

    def dev(zz, yy, xx, cc):
        return (zz * NY + yy, xx * 2 + cc)

    def zmod(v):
        return lax.rem(v + 2 * NZ, NZ)

    def zdev(o):
        return dev(zmod(z + o), y, x, core)

    xdev = [dev(z, y, lax.rem(x + d, NX), core) for d in (1, 2, 3)]
    ydev = [dev(z, lax.rem(y + d, NY), x, core) for d in (1, 2, 3)]
    cdev = dev(z, y, x, 1 - core)

    barrier = pltpu.get_barrier_semaphore()
    peers = [zdev(o) for o in (5, -5, 3, -3, 2, -2, 1, -1)] + xdev + ydev + [cdev]
    for p in peers:
        pl.semaphore_signal(barrier, inc=1, device_id=p, device_id_type=MESH)
    loads = [pltpu.make_async_copy(a, b, lsem.at[i]) for i, (a, b) in enumerate(
        ((rp_hbm, rp), (dt_hbm, dt), (lp_hbm, lp), (lr_hbm, lr_raw), (rr_hbm, rr)))]
    for ld in loads:
        ld.start()

    pending = []

    def rows_of(zz):
        return pl.ds(pl.multiple_of(zz * 32, 32), 32)

    def remote(src, dst, send, recv, to):
        cp = pltpu.make_async_remote_copy(src, dst, send, recv, device_id=to, device_id_type=MESH)
        cp.start()
        pending.append(cp)

    def arrive(dst, send, recv, to):
        pltpu.make_async_remote_copy(dst, dst, send, recv, device_id=to, device_id_type=MESH).wait_recv()

    def mat_slice(s, zz):
        return mats.at[pl.ds(STARTS[s], LENS[s]), rows_of(zz), :]

    def send_mat(s, way, k):
        sl = mat_slice(s, zmod(z - k) if way == 0 else zmod(z + k))
        remote(sl, sl, msend.at[s, way, k], mrecv.at[s, way, k], zdev(1 - 2 * way))

    def first(s):
        send_mat(s, 0, 0)
        send_mat(s, 1, 0)

    def relay(s, k):
        for way, last in ((0, 8), (1, 7)):
            if 1 <= k <= last:
                sl = mat_slice(s, zmod(z - k) if way == 0 else zmod(z + k))
                arrive(sl, msend.at[s, way, k - 1], mrecv.at[s, way, k - 1], zdev(1 - 2 * way))
                if k < last:
                    send_mat(s, way, k)

    quarter = pl.ds(pl.multiple_of(lax.rem(y, 2) * 16, 16), 16)

    def piece(w, zz):
        if w == 0:
            return xg.at[zz, y // 2, quarter, :]
        if w < 4:
            return xg.at[zz, w]
        return bm.at[w - 4, rows_of(zz), :] if w < 6 else mat_slice(w - 6, zz)

    def push(w, i, o, shard):
        sl = piece(w, zmod(z + shard))
        remote(sl, sl, wsend.at[w, i], wrecv.at[w, i], zdev(o))

    def got(w, i, o, shard):
        arrive(piece(w, zmod(z - o + shard)), wsend.at[w, i], wrecv.at[w, i], zdev(o))

    PASS = [(0, -5, (2, -2, 1, -1), 6), (1, 5, (-3, -2, 2, -1, 1), 10)]

    def wave_a(w):
        for i, o in enumerate(OWN_HOPS):
            push(w, i, o, 0)

    def wave_b(w):
        for i, shard, hops, base in PASS:
            got(w, i, OWN_HOPS[i], 0)
            for j, o in enumerate(hops):
                push(w, base + j, o, shard)

    def wave_c(w):
        for i in range(2, 6):
            got(w, i, OWN_HOPS[i], 0)
        for i, shard, hops, base in PASS:
            for j, o in enumerate(hops):
                got(w, base + j, o, shard)

    base_n = lax.rem(z, 2) * 32
    lane = lax.broadcasted_iota(jnp.int32, (32, 128), 1)
    row = lax.broadcasted_iota(jnp.int32, (32, 128), 0)
    owner = z // 2 == c

    def pick(s):
        hit = jnp.logical_and(lane == row + ((s % 2) * 64 + base_n), jnp.broadcast_to(owner, lane.shape))
        return jnp.where(hit, 1.0, 0.0).astype(BF)

    def step_p(s):
        part = dot_t(pick(s), bm[s // 2])
        for t in range(s):
            part = part - dot_t(xl[t], mats[STARTS[s] + 1 + t])
        csend[s] = part.astype(BF)
        remote(csend.at[s], crecv.at[s], csem.at[0, s], csem.at[1, s], cdev)

    def step_x(s):
        arrive(crecv.at[s], csem.at[0, s], csem.at[1, s], cdev)
        xbuf[s, x] = (csend[s].astype(F32) + crecv[s].astype(F32)).astype(BF)
        for d in (2, 1, 3):
            remote(xbuf.at[s, x], xbuf.at[s, x], xsem.at[0, s, d - 1], xsem.at[1, s, d - 1], xdev[d - 1])

    def step_y(s):
        for d in (1, 3, 2):
            arrive(xbuf.at[s, lax.rem(x + NX - d, NX)], xsem.at[0, s, d - 1], xsem.at[1, s, d - 1], xdev[d - 1])
        total = xbuf[s, 0].astype(F32)
        for i in range(1, NX):
            total = total + xbuf[s, i].astype(F32)
        prod = jnp.dot(total.astype(BF), mats[STARTS[s]], preferred_element_type=F32)
        ybuf[s, y] = prod.astype(BF)
        for d in (2, 1, 3):
            remote(ybuf.at[s, y], ybuf.at[s, y], ysem.at[0, s, d - 1], ysem.at[1, s, d - 1], ydev[d - 1])

    def step_z(s):
        for d in (1, 3, 2):
            arrive(ybuf.at[s, lax.rem(y + NY - d, NY)], ysem.at[0, s, d - 1], ysem.at[1, s, d - 1], ydev[d - 1])
        solved = ybuf[s, 0].astype(F32)
        for i in range(1, NY):
            solved = solved + ybuf[s, i].astype(F32)
        xl[s] = solved.astype(BF)
        if s == 1:
            xg[z, y // 2, quarter, :] = xl[y // 2, quarter, :]
            wave_a(0)
        elif s > 1:
            xg[z, s] = xl[s]
            wave_a(s)

    def share_slice(yy):
        return xg.at[:, yy // 2, pl.ds(pl.multiple_of(lax.rem(yy, 2) * 16, 16), 16), :]

    def share():
        for d in (2, 1, 3):
            remote(share_slice(y), share_slice(y), qsem.at[0, d - 1], qsem.at[1, d - 1], ydev[d - 1])

    def shared():
        for d in (1, 3, 2):
            arrive(share_slice(lax.rem(y + NY - d, NY)), qsem.at[0, d - 1], qsem.at[1, d - 1], ydev[d - 1])

    def tile(i):
        rows = pl.ds(i * 128, 128)
        for t in range(4):
            lr[rows, t * 256:(t + 1) * 256] = lr_raw[rows, t, :]

    loads[0].wait()
    for s in range(4):
        bm[s // 2, rows_of(z), (s % 2) * 64:(s % 2) * 64 + 64] = rp[s]
    loads[1].wait()
    loads[2].wait()
    for s in range(4):
        mats[STARTS[s], rows_of(z), :] = dt[s]
        for t in range(s):
            mats[STARTS[s] + 1 + t, rows_of(z), :] = lp[s, :, t, :]
    pl.semaphore_wait(barrier, len(peers))

    wave_a(4)
    wave_a(6)
    first(1)
    first(2)
    first(3)
    loads[3].wait()
    tile(0)
    tile(1)
    tile(2)
    tile(3)
    wave_b(4)
    wave_b(6)
    relay(1, 1)
    relay(2, 1)
    relay(3, 1)
    tile(4)
    relay(1, 2)
    relay(2, 2)
    relay(3, 2)
    tile(5)
    wave_c(4)
    step_p(0)
    relay(1, 3)
    relay(2, 3)
    relay(3, 3)
    step_x(0)
    relay(1, 4)
    relay(2, 4)
    relay(3, 4)
    wave_c(6)
    step_y(0)
    relay(1, 5)
    relay(2, 5)
    relay(3, 5)
    step_z(0)
    relay(1, 6)
    relay(2, 6)
    relay(3, 6)
    wave_a(5)
    relay(1, 7)
    relay(2, 7)
    relay(3, 7)
    relay(1, 8)
    step_p(1)
    wave_b(5)
    step_x(1)
    tile(6)
    tile(7)
    step_y(1)
    relay(2, 8)
    wave_c(5)
    step_z(1)
    step_p(2)
    tile(8)
    step_x(2)
    wave_b(0)
    tile(9)
    step_y(2)
    relay(3, 8)
    step_z(2)
    step_p(3)
    tile(10)
    step_x(3)
    tile(11)
    step_y(3)
    wave_c(0)
    share()
    wave_b(2)
    step_z(3)
    shared()
    for i in range(4):
        rows = pl.ds(i * 128, 128)
        part = None
        for t in range(2):
            term = dot_t(xg[i * 4:i * 4 + 4, t].reshape(128, 256), lr[:, t * 256:(t + 1) * 256])
            part = term if part is None else part + term
        acc[rows, :] = part
    for g in range(4):
        for t in range(2):
            sol[t, :, g * 128:(g + 1) * 128] = xg[g * 4:g * 4 + 4, t].reshape(128, 256).T
    wave_b(3)
    wave_c(2)
    for i in range(4):
        rows = pl.ds(i * 128, 128)
        acc[rows, :] += dot_t(xg[i * 4:i * 4 + 4, 2].reshape(128, 256), lr[:, 512:768])
    for g in range(4):
        sol[2, :, g * 128:(g + 1) * 128] = xg[g * 4:g * 4 + 4, 2].reshape(128, 256).T
    wave_c(3)

    mine = pl.ds(pl.multiple_of(core * 64, 64), 64)
    other = pl.ds(pl.multiple_of((1 - core) * 64, 64), 64)
    order = (2, 1, 3, 0)
    final = None
    for j in range(5):
        if j < 4:
            g = lax.rem(x + order[j], NX)
            rows = pl.ds(pl.multiple_of(g * 128, 128), 128)
            part = acc[rows, :] + dot_t(xg[pl.ds(g * 4, 4), 3].reshape(128, 256), lr[:, 768:1024])
            fsend[j] = part.astype(BF)
            remote(fsend.at[j, other], frecv.at[j], fsem.at[0, j], fsem.at[1, j], cdev)
        if j:
            i, e = j - 1, order[j - 1]
            arrive(frecv.at[i], fsem.at[0, i], fsem.at[1, i], cdev)
            chip = fsend[i, mine].astype(F32) + frecv[i].astype(F32)
            if e:
                rsend[i] = chip.astype(BF)
                remote(rsend.at[i], rbuf.at[e - 1], rsem.at[0, e - 1], rsem.at[1, e - 1], xdev[e - 1])
            else:
                loads[4].wait()
                final = rr[...].astype(F32) - chip
    for g in range(4):
        sol[3, :, g * 128:(g + 1) * 128] = xg[g * 4:g * 4 + 4, 3].reshape(128, 256).T
    for e in (1, 3, 2):
        arrive(rbuf.at[e - 1], rsem.at[0, e - 1], rsem.at[1, e - 1], xdev[e - 1])
        final = final - rbuf[e - 1].astype(F32)
    rem[...] = final.astype(BF)
    for cp in pending:
        cp.wait_send()


def per_device(lower_pivot, lower_rest, diag_inverse, rhs_pivot, rhs_rest):
    vmem = pl.BlockSpec(memory_space=pltpu.VMEM)
    hbm = pl.BlockSpec(memory_space=pltpu.HBM)
    dma = pltpu.SemaphoreType.DMA
    return pl.pallas_call(
        kernel,
        out_shape=(jax.ShapeDtypeStruct((4, 256, 512), BF), jax.ShapeDtypeStruct((64, 1536), BF)),
        in_specs=[hbm] * 5,
        out_specs=(vmem, vmem),
        scratch_shapes=[
            pltpu.VMEM((4, 32, 4, 256), BF),
            pltpu.VMEM((4, 32, 256), BF),
            pltpu.VMEM((4, 32, 64), BF),
            pltpu.VMEM((64, 1536), BF),
            pltpu.VMEM((1536, 4, 256), BF),
            pltpu.VMEM((1536, 1024), BF),
            pltpu.VMEM((BLOCKS, 512, 256), BF),
            pltpu.VMEM((2, 512, 128), BF),
            pltpu.VMEM((NZ, 4, 32, 256), BF),
            pltpu.VMEM((4, 32, 256), BF),
            pltpu.VMEM((4, 32, 512), BF),
            pltpu.VMEM((4, 32, 512), BF),
            pltpu.VMEM((4, 4, 32, 512), BF),
            pltpu.VMEM((4, 4, 32, 256), BF),
            pltpu.VMEM((512, 1536), F32),
            pltpu.VMEM((4, 128, 1536), BF),
            pltpu.VMEM((4, 64, 1536), BF),
            pltpu.VMEM((3, 64, 1536), BF),
            pltpu.VMEM((3, 64, 1536), BF),
            dma((5,)),
            dma((4, 2, 8)),
            dma((4, 2, 8)),
            dma((8, 15)),
            dma((8, 15)),
            dma((2, 4)),
            dma((2, 4, 3)),
            dma((2, 4, 3)),
            dma((2, 3)),
            dma((2, 4)),
            dma((2, 3)),
        ],
        compiler_params=pltpu.CompilerParams(
            collective_id=0, has_side_effects=True, vmem_limit_bytes=63 * 1024 * 1024
        ),
        name="substitution",
    )(lower_pivot, jnp.swapaxes(diag_inverse, 1, 2), rhs_pivot, rhs_rest, lower_rest)


def solution(mesh):
    placed = (
        P(None, "rows", None, "cols"),
        P("rows", None, "cols"),
        P(None, "cols", "rows"),
        P(None, "rows", "cols"),
        P("cols", "rows"),
    )
    return jax.shard_map(
        per_device,
        mesh=mesh,
        in_specs=placed,
        out_specs=(P(None, "cols", None), P("cols", "rows")),
        check_vma=False,
    )
```

```python
import jax
import jax.numpy as jnp
from jax import lax
from jax.experimental import pallas as pl
from jax.experimental.pallas import tpu as pltpu
from jax.sharding import PartitionSpec as P

MESH = pl.DeviceIdType.MESH
BF = jnp.bfloat16
F32 = jnp.float32
NZ, NY, NX = 16, 4, 4
STARTS = (0, 1, 3, 6)
LENS = (1, 2, 3, 4)
BLOCKS = 10
OWN_HOPS = (5, -5, 2, -2, 1, -1)
CONTRACT_LAST = (((1,), (1,)), ((), ()))


def dot_t(a, b):
    return lax.dot_general(a, b, CONTRACT_LAST, preferred_element_type=F32)


def kernel(lp_hbm, dt_hbm, rp_hbm, rr_hbm, lr_hbm, sol, rem,
           lp, dt, rp, rr, lr_raw, lr, mats, bm, xg, xl, csend, crecv, xbuf, ybuf, acc, fsend, frecv, rsend, rbuf,
           lsem, msend, mrecv, wsend, wrecv, csem, xsem, ysem, qsem, fsem, rsem):
    r = lax.axis_index("rows")
    c = lax.axis_index("cols")
    z, y = r // NY, lax.rem(r, NY)
    x, core = c // 2, lax.rem(c, 2)

    def dev(zz, yy, xx, cc):
        return (zz * NY + yy, xx * 2 + cc)

    def zmod(v):
        return lax.rem(v + 2 * NZ, NZ)

    def zdev(o):
        return dev(zmod(z + o), y, x, core)

    xdev = [dev(z, y, lax.rem(x + d, NX), core) for d in (1, 2, 3)]
    ydev = [dev(z, lax.rem(y + d, NY), x, core) for d in (1, 2, 3)]
    cdev = dev(z, y, x, 1 - core)

    barrier = pltpu.get_barrier_semaphore()
    peers = [zdev(o) for o in (5, -5, 3, -3, 2, -2, 1, -1)] + xdev + ydev + [cdev]
    for p in peers:
        pl.semaphore_signal(barrier, inc=1, device_id=p, device_id_type=MESH)
    loads = [pltpu.make_async_copy(a, b, lsem.at[i]) for i, (a, b) in enumerate(
        ((rp_hbm, rp), (dt_hbm, dt), (lp_hbm, lp), (lr_hbm, lr_raw), (rr_hbm, rr)))]
    for ld in loads:
        ld.start()

    pending = []

    def rows_of(zz):
        return pl.ds(pl.multiple_of(zz * 32, 32), 32)

    def remote(src, dst, send, recv, to):
        cp = pltpu.make_async_remote_copy(src, dst, send, recv, device_id=to, device_id_type=MESH)
        cp.start()
        pending.append(cp)

    def arrive(dst, send, recv, to):
        pltpu.make_async_remote_copy(dst, dst, send, recv, device_id=to, device_id_type=MESH).wait_recv()

    def mat_slice(s, zz):
        return mats.at[pl.ds(STARTS[s], LENS[s]), rows_of(zz), :]

    def send_mat(s, way, k):
        sl = mat_slice(s, zmod(z - k) if way == 0 else zmod(z + k))
        remote(sl, sl, msend.at[s, way, k], mrecv.at[s, way, k], zdev(1 - 2 * way))

    def first(s):
        send_mat(s, 0, 0)
        send_mat(s, 1, 0)

    def relay(s, k):
        for way, last in ((0, 8), (1, 7)):
            if 1 <= k <= last:
                sl = mat_slice(s, zmod(z - k) if way == 0 else zmod(z + k))
                arrive(sl, msend.at[s, way, k - 1], mrecv.at[s, way, k - 1], zdev(1 - 2 * way))
                if k < last:
                    send_mat(s, way, k)

    quarter = pl.ds(pl.multiple_of(lax.rem(y, 2) * 16, 16), 16)

    def piece(w, zz):
        if w == 0:
            return xg.at[zz, y // 2, quarter, :]
        if w < 4:
            return xg.at[zz, w]
        return bm.at[w - 4, rows_of(zz), :] if w < 6 else mat_slice(w - 6, zz)

    def push(w, i, o, shard):
        sl = piece(w, zmod(z + shard))
        remote(sl, sl, wsend.at[w, i], wrecv.at[w, i], zdev(o))

    def got(w, i, o, shard):
        arrive(piece(w, zmod(z - o + shard)), wsend.at[w, i], wrecv.at[w, i], zdev(o))

    PASS = [(0, -5, (2, -2, 1, -1), 6), (1, 5, (-3, -2, 2, -1, 1), 10)]

    def wave_a(w):
        for i, o in enumerate(OWN_HOPS):
            push(w, i, o, 0)

    def wave_b(w):
        for i, shard, hops, base in PASS:
            got(w, i, OWN_HOPS[i], 0)
            for j, o in enumerate(hops):
                push(w, base + j, o, shard)

    def wave_c(w):
        for i in range(2, 6):
            got(w, i, OWN_HOPS[i], 0)
        for i, shard, hops, base in PASS:
            for j, o in enumerate(hops):
                got(w, base + j, o, shard)

    base_n = lax.rem(z, 2) * 32
    lane = lax.broadcasted_iota(jnp.int32, (32, 128), 1)
    row = lax.broadcasted_iota(jnp.int32, (32, 128), 0)
    owner = z // 2 == c

    def pick(s):
        hit = jnp.logical_and(lane == row + ((s % 2) * 64 + base_n), jnp.broadcast_to(owner, lane.shape))
        return jnp.where(hit, 1.0, 0.0).astype(BF)

    def step_p(s):
        part = dot_t(pick(s), bm[s // 2])
        for t in range(s):
            part = part - dot_t(xl[t], mats[STARTS[s] + 1 + t])
        csend[s] = part.astype(BF)
        remote(csend.at[s], crecv.at[s], csem.at[0, s], csem.at[1, s], cdev)

    def step_x(s):
        arrive(crecv.at[s], csem.at[0, s], csem.at[1, s], cdev)
        xbuf[s, x] = (csend[s].astype(F32) + crecv[s].astype(F32)).astype(BF)
        for d in (2, 1, 3):
            remote(xbuf.at[s, x], xbuf.at[s, x], xsem.at[0, s, d - 1], xsem.at[1, s, d - 1], xdev[d - 1])

    def step_y(s):
        for d in (1, 3, 2):
            arrive(xbuf.at[s, lax.rem(x + NX - d, NX)], xsem.at[0, s, d - 1], xsem.at[1, s, d - 1], xdev[d - 1])
        total = xbuf[s, 0].astype(F32)
        for i in range(1, NX):
            total = total + xbuf[s, i].astype(F32)
        prod = jnp.dot(total.astype(BF), mats[STARTS[s]], preferred_element_type=F32)
        ybuf[s, y] = prod.astype(BF)
        for d in (2, 1, 3):
            remote(ybuf.at[s, y], ybuf.at[s, y], ysem.at[0, s, d - 1], ysem.at[1, s, d - 1], ydev[d - 1])

    def step_z(s):
        for d in (1, 3, 2):
            arrive(ybuf.at[s, lax.rem(y + NY - d, NY)], ysem.at[0, s, d - 1], ysem.at[1, s, d - 1], ydev[d - 1])
        solved = ybuf[s, 0].astype(F32)
        for i in range(1, NY):
            solved = solved + ybuf[s, i].astype(F32)
        xl[s] = solved.astype(BF)
        if s == 1:
            xg[z, y // 2, quarter, :] = xl[y // 2, quarter, :]
            wave_a(0)
        elif s > 1:
            xg[z, s] = xl[s]
            wave_a(s)

    def share_slice(yy):
        return xg.at[:, yy // 2, pl.ds(pl.multiple_of(lax.rem(yy, 2) * 16, 16), 16), :]

    def share():
        for d in (2, 1, 3):
            remote(share_slice(y), share_slice(y), qsem.at[0, d - 1], qsem.at[1, d - 1], ydev[d - 1])

    def shared():
        for d in (1, 3, 2):
            arrive(share_slice(lax.rem(y + NY - d, NY)), qsem.at[0, d - 1], qsem.at[1, d - 1], ydev[d - 1])

    def tile(i):
        rows = pl.ds(i * 128, 128)
        for t in range(4):
            lr[rows, t * 256:(t + 1) * 256] = lr_raw[rows, t, :]

    loads[0].wait()
    for s in range(4):
        bm[s // 2, rows_of(z), (s % 2) * 64:(s % 2) * 64 + 64] = rp[s]
    loads[1].wait()
    loads[2].wait()
    for s in range(4):
        mats[STARTS[s], rows_of(z), :] = dt[s]
        for t in range(s):
            mats[STARTS[s] + 1 + t, rows_of(z), :] = lp[s, :, t, :]
    pl.semaphore_wait(barrier, len(peers))

    wave_a(4)
    wave_a(6)
    first(2)
    loads[3].wait()
    tile(0)
    tile(1)
    tile(2)
    tile(3)
    wave_b(4)
    wave_b(6)
    wave_a(7)
    relay(2, 1)
    first(3)
    tile(4)
    tile(5)
    tile(6)
    wave_c(4)
    step_p(0)
    relay(2, 2)
    step_x(0)
    wave_b(7)
    relay(3, 1)
    wave_c(6)
    step_y(0)
    wave_a(5)
    relay(2, 3)
    relay(3, 2)
    step_z(0)
    wave_c(7)
    step_p(1)
    relay(2, 4)
    step_x(1)
    wave_b(5)
    relay(3, 3)
    relay(2, 5)
    step_y(1)
    relay(3, 4)
    relay(2, 6)
    step_z(1)
    relay(2, 7)
    relay(3, 5)
    relay(2, 8)
    wave_c(5)
    step_p(2)
    relay(3, 6)
    step_x(2)
    wave_b(0)
    relay(3, 7)
    tile(7)
    tile(8)
    step_y(2)
    relay(3, 8)
    step_z(2)
    step_p(3)
    wave_c(0)
    share()
    tile(9)
    step_x(3)
    tile(10)
    tile(11)
    step_y(3)
    wave_b(2)
    step_z(3)
    shared()
    for i in range(4):
        rows = pl.ds(i * 128, 128)
        part = None
        for t in range(2):
            term = dot_t(xg[i * 4:i * 4 + 4, t].reshape(128, 256), lr[:, t * 256:(t + 1) * 256])
            part = term if part is None else part + term
        acc[rows, :] = part
    wave_b(3)
    wave_c(2)
    for i in range(4):
        rows = pl.ds(i * 128, 128)
        acc[rows, :] += dot_t(xg[i * 4:i * 4 + 4, 2].reshape(128, 256), lr[:, 512:768])
    wave_c(3)

    mine = pl.ds(pl.multiple_of(core * 64, 64), 64)
    other = pl.ds(pl.multiple_of((1 - core) * 64, 64), 64)
    order = (2, 1, 3, 0)
    final = None
    for j in range(5):
        if j < 4:
            g = lax.rem(x + order[j], NX)
            rows = pl.ds(pl.multiple_of(g * 128, 128), 128)
            part = acc[rows, :] + dot_t(xg[pl.ds(g * 4, 4), 3].reshape(128, 256), lr[:, 768:1024])
            fsend[j] = part.astype(BF)
            remote(fsend.at[j, other], frecv.at[j], fsem.at[0, j], fsem.at[1, j], cdev)
        if j:
            i, e = j - 1, order[j - 1]
            arrive(frecv.at[i], fsem.at[0, i], fsem.at[1, i], cdev)
            chip = fsend[i, mine].astype(F32) + frecv[i].astype(F32)
            if e:
                rsend[i] = chip.astype(BF)
                remote(rsend.at[i], rbuf.at[e - 1], rsem.at[0, e - 1], rsem.at[1, e - 1], xdev[e - 1])
            else:
                loads[4].wait()
                final = rr[...].astype(F32) - chip
    for g in range(4):
        for t in range(4):
            sol[t, :, g * 128:(g + 1) * 128] = xg[g * 4:g * 4 + 4, t].reshape(128, 256).T
    for e in (1, 3, 2):
        arrive(rbuf.at[e - 1], rsem.at[0, e - 1], rsem.at[1, e - 1], xdev[e - 1])
        final = final - rbuf[e - 1].astype(F32)
    rem[...] = final.astype(BF)
    for cp in pending:
        cp.wait_send()


def per_device(lower_pivot, lower_rest, diag_inverse, rhs_pivot, rhs_rest):
    vmem = pl.BlockSpec(memory_space=pltpu.VMEM)
    hbm = pl.BlockSpec(memory_space=pltpu.HBM)
    dma = pltpu.SemaphoreType.DMA
    return pl.pallas_call(
        kernel,
        out_shape=(jax.ShapeDtypeStruct((4, 256, 512), BF), jax.ShapeDtypeStruct((64, 1536), BF)),
        in_specs=[hbm] * 5,
        out_specs=(vmem, vmem),
        scratch_shapes=[
            pltpu.VMEM((4, 32, 4, 256), BF),
            pltpu.VMEM((4, 32, 256), BF),
            pltpu.VMEM((4, 32, 64), BF),
            pltpu.VMEM((64, 1536), BF),
            pltpu.VMEM((1536, 4, 256), BF),
            pltpu.VMEM((1536, 1024), BF),
            pltpu.VMEM((BLOCKS, 512, 256), BF),
            pltpu.VMEM((2, 512, 128), BF),
            pltpu.VMEM((NZ, 4, 32, 256), BF),
            pltpu.VMEM((4, 32, 256), BF),
            pltpu.VMEM((4, 32, 512), BF),
            pltpu.VMEM((4, 32, 512), BF),
            pltpu.VMEM((4, 4, 32, 512), BF),
            pltpu.VMEM((4, 4, 32, 256), BF),
            pltpu.VMEM((512, 1536), F32),
            pltpu.VMEM((4, 128, 1536), BF),
            pltpu.VMEM((4, 64, 1536), BF),
            pltpu.VMEM((3, 64, 1536), BF),
            pltpu.VMEM((3, 64, 1536), BF),
            dma((5,)),
            dma((4, 2, 8)),
            dma((4, 2, 8)),
            dma((8, 15)),
            dma((8, 15)),
            dma((2, 4)),
            dma((2, 4, 3)),
            dma((2, 4, 3)),
            dma((2, 3)),
            dma((2, 4)),
            dma((2, 3)),
        ],
        compiler_params=pltpu.CompilerParams(
            collective_id=0, has_side_effects=True, vmem_limit_bytes=63 * 1024 * 1024
        ),
        name="substitution",
    )(lower_pivot, jnp.swapaxes(diag_inverse, 1, 2), rhs_pivot, rhs_rest, lower_rest)


def solution(mesh):
    placed = (
        P(None, "rows", None, "cols"),
        P("rows", None, "cols"),
        P(None, "cols", "rows"),
        P(None, "rows", "cols"),
        P("cols", "rows"),
    )
    return jax.shard_map(
        per_device,
        mesh=mesh,
        in_specs=placed,
        out_specs=(P(None, "cols", None), P("cols", "rows")),
        check_vma=False,
    )
```
